32 devices in a mesh: band: 8 (over z, x), tile: 4 (over y, core).
Axes of the slice: x: 2, y: 2, z: 4, core: 2. Of those that a mesh axis runs over, the one named last changes fastest.
Arguments:
- source: bfloat16 [40, 262144], P(None, ('band', 'tile')), may hold values from -6 to 6
- regrid_weights: bfloat16 [2048, 4, 128, 128], P(('band', 'tile')), may hold values from -0.5 to 0.5
- dest_group: int32 [2048, 4], P(('band', 'tile')), may hold values from 0 to 31, all different within a row; in each aligned block of 64 rows (0 to 63, 64 to 127, ...) at most 24 rows name the same one
- dest_block: int32 [2048, 4], P(('band', 'tile')), may hold values from 0 to 767
- seam_table: int32 [12, 4, 3], replicated, may hold values from 0 to 11, as said below
- conv1_weight: bfloat16 [9, 128, 40], replicated, may hold values from -0.3125 to 0.3125
- conv1_bias: float32 [128], replicated, may hold values from -3 to 3
- conv2_weight: bfloat16 [9, 128, 128], replicated, may hold values from -0.1875 to 0.1875
- conv2_bias: float32 [128], replicated, may hold values from -3 to 3
Outputs:
- features: bfloat16 [128, 12, 512, 512], P(None, None, 'band', 'tile')
The draws below stay inside these ranges and needn't reach their ends.
Inputs may be any that keep to these rules, and one draw needn't show every extreme that they name: `dest_group`: within the rows of one device (aligned blocks of 64 rows) no value appears more than 24 times, and a row's 4 values differ. `seam_table`: entries 0 and 1 name a face and a side (0 to 3). Joins are symmetric: if side s of face f is joined to side s2 of face g, side s2 of face g is joined to side s of face f with the same reversal entry. No side is joined to itself. Entry 2 is 0 or 1.
All inputs are finite; a program needn't handle non-finite values.
Results may differ from the reference program's by a relative error of at most 0.0058.
Values may be sent and summed in bfloat16 or wider, within the bound.
A program may use at most 640 MiB of HBM per device.

```python
import math
import jax
import jax.numpy as jnp
import numpy as np
from jax import lax

FIELDS = 40
HID = 128
BLK = 128
FACES = 12
KB = 4
SB_DEV = 64
C = 24
NSIDE = 512
ROWS_DEV = 64
TB_DEV = 768
SRC_BLOCKS = 2048
SRC_CELLS = 262144
N_BAND = 8
N_TILE = 4
DEVICES = 32


def draw_seam_table(key, part):
    order = jax.random.permutation(key, 4 * FACES).astype(jnp.int32)
    firsts = order[0::2]
    seconds = order[1::2]
    partner = jnp.zeros((4 * FACES,), jnp.int32).at[firsts].set(seconds).at[seconds].set(firsts)
    flips = jax.random.randint(jax.random.fold_in(key, 7), (2 * FACES,), 0, 2).astype(jnp.int32)
    reverse = jnp.zeros((4 * FACES,), jnp.int32).at[firsts].set(flips).at[seconds].set(flips)
    return jnp.stack((partner // 4, partner % 4, reverse), axis=1).reshape(FACES, 4, 3).astype(jnp.int32)


def with_ends(values, own_key, low, high):
    extent = values.shape
    place = [jax.random.randint(jax.random.fold_in(own_key, axis), (), 0, extent[axis]) for axis in range(len(extent))]
    values = values.at[tuple(place)].set(low)
    longest = extent.index(max(extent))
    place[longest] = (place[longest] + 1) % extent[longest]
    return values.at[tuple(place)].set(high)


def block_scale(own_key, extent, pieces, smallest, largest):
    loudness = 1.0
    for position, shards_of in pieces:
        heights = jax.random.uniform(jax.random.fold_in(jax.random.fold_in(own_key, 6), position), (shards_of,), jnp.float32, smallest / len(pieces), largest / len(pieces))
        loudness = loudness * jnp.repeat(jnp.exp(heights), extent[position] // shards_of).reshape((-1,) + (1,) * (len(extent) - 1 - position))
    return loudness


def routed_block(rng, own, number, rows, number_of, top, limit, lean):
    sequence = jax.random.permutation(rng, number_of)
    heavy_load, common = portions_of(number_of, rows * top, limit, lean, True), portions_of(number_of, rows * top, limit, lean, False)
    places = jnp.arange(number_of)

    def named(sizes, turn):
        used = int((sizes > 0).sum())
        fixed = max(1, used // 4)
        shifted = fixed + (places - fixed + turn * (used - fixed)) % max(1, number_of - fixed)
        return jnp.zeros((number_of,), jnp.int32).at[sequence[jnp.where(places < fixed, places, shifted)]].set(jnp.asarray(sizes, jnp.int32))

    sizes = jnp.where(number % 4 == 0, named(heavy_load, number // 4), named(common, number - number // 4 - 1))
    mixed = jax.random.permutation(jax.random.fold_in(own, 3), number_of)
    source_of, taker = mixed[0:number_of // 2 * 2:2], mixed[1:number_of // 2 * 2:2]
    room = jnp.minimum(sizes[source_of] - 1, limit - sizes[taker]) // 2
    room = jnp.where((source_of == sequence[0]) | (taker == sequence[0]) | (sizes[taker] == 0), 0, jnp.maximum(room, 0))
    shifted = jax.random.randint(jax.random.fold_in(own, 4), (number_of // 2,), 0, 1 << 20) % (room + 1)
    sizes = sizes.at[source_of].add(-shifted).at[taker].add(shifted)
    items = jnp.searchsorted(jnp.cumsum(sizes), jnp.arange(rows * top), side="right").astype(jnp.int32)
    listing = items.reshape(top, rows).T
    listing = listing[jax.random.permutation(jax.random.fold_in(own, 1), rows)]
    turn = jax.random.randint(jax.random.fold_in(own, 2), (rows, 1), 0, top)
    return jnp.take_along_axis(listing, (jnp.arange(top)[None, :] + turn) % top, axis=1)


def portions_of(amount, total, limit, slope, full):
    portions = [(1 << 20) // math.isqrt(rank ** slope) + 1 for rank in range(1, amount + 1)]
    largest = limit if full else min(limit, max(-(-total // amount), total * portions[0] // sum(portions)))
    least = 1 if total - largest >= amount - 1 else 0
    holding, spare = [largest] + [least] * (amount - 1), total - largest - least * (amount - 1)
    while spare > 0:
        candidates = [i for i in range(1, amount) if holding[i] < largest] or [i for i in range(1, amount) if holding[i] < limit]
        pool, remaining = sum([portions[i] for i in candidates]), spare
        for i in candidates:
            addition = min(limit - holding[i], max(1, remaining * portions[i] // pool), spare)
            holding[i] = holding[i] + addition
            spare = spare - addition
    return np.array(holding)


def noise(rng, dims, scale, reach, pieces=(), held_as=jnp.bfloat16):
    entries = jax.random.normal(rng, dims, jnp.float32) * scale
    if len(pieces) > 0:
        entries = block_scale(rng, dims, pieces, -0.22, 0.18) * entries
    return jnp.clip(entries, min=-reach, max=reach).astype(held_as)


def setup_inputs(seed: int = 0) -> dict:
    seeds = jax.random.split(jax.random.key(seed), 10)
    source = noise(seeds[0], (FIELDS, SRC_CELLS), 1.0, 6.0, ((1, 32),))
    regrid_weights = noise(seeds[1], (SRC_BLOCKS, KB, BLK, BLK), BLK ** -0.5, 0.5, ((0, 32),))
    dest_group_keys = jax.random.split(jax.random.fold_in(seeds[2], 1), SRC_BLOCKS // SB_DEV)
    dest_group_turns = jax.random.permutation(jax.random.fold_in(seeds[2], 3), SRC_BLOCKS // SB_DEV)
    dest_group = jax.vmap(lambda own, number: routed_block(jax.random.fold_in(seeds[2], 2), own, number, SB_DEV, DEVICES, KB, C, 1))(dest_group_keys, dest_group_turns).reshape((SRC_BLOCKS, KB))
    dest_block = with_ends(jax.random.randint(seeds[3], (SRC_BLOCKS, KB), 0, TB_DEV), jax.random.fold_in(seeds[3], 1), 0, TB_DEV - 1).astype(jnp.int32)
    seam_table = draw_seam_table(jax.random.fold_in(seeds[9], 71), 0)
    conv1_weight = noise(seeds[5], (9, HID, FIELDS), (9 * FIELDS) ** -0.5, 0.3125)
    conv1_bias = noise(seeds[6], (HID,), 0.5, 3.0, (), jnp.float32)
    conv2_weight = noise(seeds[7], (9, HID, HID), (9 * HID) ** -0.5, 0.1875)
    conv2_bias = noise(seeds[8], (HID,), 0.5, 3.0, (), jnp.float32)
    return dict(source=source, regrid_weights=regrid_weights, dest_group=dest_group, dest_block=dest_block, seam_table=seam_table, conv1_weight=conv1_weight, conv1_bias=conv1_bias, conv2_weight=conv2_weight, conv2_bias=conv2_bias)


def conv_faces(field_in, weight, bias_row, seam_table):
    channels = field_in.shape[0]
    side_len = field_in.shape[2]
    edge_lines = jnp.stack((field_in[:, :, 0, :], field_in[:, :, -1, :], field_in[:, :, :, 0], field_in[:, :, :, -1]), axis=2).reshape(channels, FACES * 4, side_len)
    line_index = (seam_table[:, :, 0] * 4 + seam_table[:, :, 1]).reshape(-1)
    reverse = (seam_table[:, :, 2] == 1).reshape(-1)[None, :, None]
    seam_lines = edge_lines[:, line_index, :]
    seam_lines = jnp.where(reverse, jnp.flip(seam_lines, axis=2), seam_lines).reshape(channels, FACES, 4, side_len)
    weight_wide = weight.astype(jnp.float32)

    def one_face(face_id):
        face_data = field_in[:, face_id]
        face_lines = seam_lines[:, face_id]
        padded = jnp.pad(face_data, ((0, 0), (1, 1), (1, 1)))
        padded = padded.at[:, 0, 1:-1].set(face_lines[:, 0])
        padded = padded.at[:, -1, 1:-1].set(face_lines[:, 1])
        padded = padded.at[:, 1:-1, 0].set(face_lines[:, 2])
        padded = padded.at[:, 1:-1, -1].set(face_lines[:, 3])
        padded = padded.astype(jnp.float32)
        summed = jnp.zeros((weight.shape[1], side_len, side_len), jnp.float32)
        for row_off in range(3):
            for col_off in range(3):
                window = padded[:, row_off:row_off + side_len, col_off:col_off + side_len]
                summed = summed + jnp.einsum("oi,irc->orc", weight_wide[3 * row_off + col_off], window)
        return jax.nn.gelu(summed + bias_row[:, None, None], approximate=False).astype(jnp.bfloat16)

    out_faces = lax.map(one_face, jnp.arange(FACES, dtype=jnp.int32))
    return jnp.transpose(out_faces, (1, 0, 2, 3))


def reference(source, regrid_weights, dest_group, dest_block, seam_table, conv1_weight, conv1_bias, conv2_weight, conv2_bias):
    devices = N_BAND * N_TILE
    group_blocks = source.reshape(FIELDS, devices, SB_DEV, BLK).transpose(1, 2, 0, 3)
    group_weights = regrid_weights.reshape(devices, SB_DEV, KB, BLK, BLK)

    def one_group(group_pair):
        blocks, weights = group_pair
        return jnp.einsum("sfc,skcd->skfd", blocks.astype(jnp.float32), weights.astype(jnp.float32)).astype(jnp.bfloat16)

    partial_value = lax.map(one_group, (group_blocks, group_weights))
    target = (dest_group * TB_DEV + dest_block).reshape(-1).astype(jnp.int32)
    summed = jax.ops.segment_sum(partial_value.reshape(-1, FIELDS, BLK).astype(jnp.float32), target, num_segments=devices * TB_DEV)
    regridded = summed.reshape(N_BAND, N_TILE, FACES, ROWS_DEV, FIELDS, BLK).transpose(4, 2, 0, 3, 1, 5).reshape(FIELDS, FACES, NSIDE, NSIDE).astype(jnp.bfloat16)
    hidden = conv_faces(regridded, conv1_weight, conv1_bias, seam_table)
    return conv_faces(hidden, conv2_weight, conv2_bias, seam_table)
```

```python
import functools

import jax
import jax.numpy as jnp
from jax import lax
from jax.experimental import pallas as pl
from jax.experimental.pallas import tpu as pltpu
from jax.sharding import PartitionSpec as P

BF = jnp.bfloat16
F32 = jnp.float32
VMEM_LIMIT = 60 * 1024 * 1024
PAIRS = 8
GELU_COEF = (
    0.7978842684146765,
    0.03633414911622174,
    -3.30267008968913e-05,
    -5.527338755532785e-05,
    3.974071022505988e-06,
    -1.3378322650770525e-07,
    1.8139281733930472e-09,
)
GELU_CAP = 30.0


def gelu(v):
    u = jnp.minimum(v * v, GELU_CAP)
    q = jnp.full_like(u, GELU_COEF[-1])
    for c in GELU_COEF[-2::-1]:
        q = q * u + c
    half = 0.5 * v
    return half + half * jnp.tanh(v * q)


def partial_kernel(pos_ref, src_ref, w_ref, out_ref):
    s = pl.program_id(0)
    per_step = w_ref.shape[0]
    top, blk = w_ref.shape[1], w_ref.shape[2]

    @pl.when(s == 0)
    def _():
        out_ref[...] = jnp.zeros_like(out_ref)

    for j in range(per_step):
        x = src_ref[:, j * blk : (j + 1) * blk]
        for k in range(top):
            y = jnp.dot(x, w_ref[j, k], preferred_element_type=F32).astype(BF)
            out_ref[pos_ref[(s * per_step + j) * top + k]] = y


def partials(position, source, weights, slots):
    fields = source.shape[0]
    src_count, top, blk, _ = weights.shape
    step = 4
    return pl.pallas_call(
        partial_kernel,
        out_shape=jax.ShapeDtypeStruct((slots, fields, blk), BF),
        grid_spec=pltpu.PrefetchScalarGridSpec(
            num_scalar_prefetch=1,
            grid=(src_count // step,),
            in_specs=[
                pl.BlockSpec((fields, step * blk), lambda i, p: (0, i)),
                pl.BlockSpec((step, top, blk, blk), lambda i, p: (i, 0, 0, 0)),
            ],
            out_specs=pl.BlockSpec((slots, fields, blk), lambda i, p: (0, 0, 0)),
        ),
        compiler_params=pltpu.CompilerParams(vmem_limit_bytes=VMEM_LIMIT),
        name="partials",
    )(position, source, weights)


def collect_kernel(slot_ref, arr_ref, out_ref, acc_ref):
    i = pl.program_id(0)
    n = arr_ref.shape[0]

    @pl.when(i == 0)
    def _():
        acc_ref[...] = jnp.zeros_like(acc_ref)

    def body(j, _):
        slot = slot_ref[i * n + j]
        acc_ref[slot] = acc_ref[slot] + arr_ref[j].astype(F32)
        return 0

    lax.fori_loop(0, n, body, 0, unroll=4)

    @pl.when(i == pl.num_programs(0) - 1)
    def _():
        out_ref[...] = acc_ref[: out_ref.shape[0]].astype(BF)


def collect(slots, arrived, slots_dev):
    count, fields, blk = arrived.shape
    steps = 8
    return pl.pallas_call(
        collect_kernel,
        out_shape=jax.ShapeDtypeStruct((slots_dev, fields, blk), BF),
        grid_spec=pltpu.PrefetchScalarGridSpec(
            num_scalar_prefetch=1,
            grid=(steps,),
            in_specs=[pl.BlockSpec((count // steps, fields, blk), lambda i, p: (i, 0, 0))],
            out_specs=pl.BlockSpec((slots_dev, fields, blk), lambda i, p: (0, 0, 0)),
            scratch_shapes=[pltpu.VMEM((slots_dev + 1, fields, blk), F32)],
        ),
        compiler_params=pltpu.CompilerParams(vmem_limit_bytes=VMEM_LIMIT),
        name="collect",
    )(slots, arrived)


def conv_kernel(
    first, x_ref, top_ref, bot_ref, left_ref, right_ref, wa_ref, wb_ref, b_ref, out_ref, *scratch
):
    sl, win = scratch[0], scratch[1]
    rows = out_ref.shape[0] if first else out_ref.shape[2]
    cols = sl.shape[1]
    width = sl.shape[2] // 2
    chan = left_ref.shape[-1]

    def put(pair, parity, row32, lo, hi):
        win[parity, 8 : 8 + cols, :] = row32
        win[parity, 7:8, :] = lo
        win[parity, 8 + cols : 9 + cols, :] = hi
        before = win[parity, 7 : 7 + cols, :]
        after = win[parity, 9 : 9 + cols, :]
        base = parity * width
        if first:
            g = before + pltpu.roll(row32, chan, 1) + pltpu.roll(after, 2 * chan, 1)
            sl[pair, :, base : base + width] = g.astype(BF)
        else:
            sl[pair, :, base : base + cols] = before.astype(BF)
            sl[pair, :, base + cols : base + 2 * cols] = row32.astype(BF)
            sl[pair, :, base + 2 * cols : base + 3 * cols] = after.astype(BF)

    def wide(v):
        if first:
            v = jnp.concatenate([v, jnp.zeros((v.shape[0], cols - chan), v.dtype)], axis=1)
        return v

    def row_at(r):
        if first:
            y = x_ref[r].astype(F32)
            y = jnp.concatenate([y, jnp.zeros((cols - chan, cols), F32)], axis=0)
            return y.T
        return x_ref[r].astype(F32)

    def halo_row(ref):
        full = wide(ref[0].astype(F32))
        return full[:cols], full[cols : cols + 1], full[cols + 1 : cols + 2]

    row, lo, hi = halo_row(top_ref)
    put(0, 0, row, lo, hi)
    row, lo, hi = halo_row(bot_ref)
    put(rows // 2, 1, row, lo, hi)

    def fill(i, _):
        for parity in range(2):
            r = 2 * i + parity
            put(
                i + parity,
                1 - parity,
                row_at(r),
                wide(left_ref[0, pl.ds(r, 1), :]),
                wide(right_ref[0, pl.ds(r, 1), :]),
            )
        return 0

    lax.fori_loop(0, rows // 2, fill, 0, unroll=2)

    def chunk(g, _):
        p0 = g * PAIRS
        a = sl[pl.ds(p0, PAIRS)].reshape(PAIRS * cols, 2 * width)
        b = sl[pl.ds(p0 + 1, PAIRS)].reshape(PAIRS * cols, 2 * width)
        y = jnp.dot(a, wa_ref[...], preferred_element_type=F32) + jnp.dot(
            b, wb_ref[...], preferred_element_type=F32
        )
        hid = y.shape[1] // 2
        if first:
            y = gelu(y + b_ref[...]).astype(BF)
            for p in range(PAIRS):
                for q in range(2):
                    out_ref[2 * (p0 + p) + q] = y[p * cols : (p + 1) * cols, q * hid : (q + 1) * hid]
        else:
            flip = scratch[2]
            n = 2 * PAIRS
            for p in range(PAIRS):
                for q in range(2):
                    part = y[p * cols : (p + 1) * cols, q * hid : (q + 1) * hid]
                    flip[pl.ds(2 * p + q, hid, stride=n), :] = part.T

            def finish(o, _):
                for j in range(8):
                    oo = o * 8 + j
                    v = flip[pl.ds(oo * n, n), :]
                    out_ref[oo, 0, pl.ds(g * n, n), :] = gelu(v + b_ref[oo]).astype(BF)
                return 0

            lax.fori_loop(0, hid // 8, finish, 0)
        return 0

    lax.fori_loop(0, rows // (2 * PAIRS), chunk, 0)


def conv(first, x, halos, weight, bias, face_count, rows, out_cols):
    top, bot, left, right = halos
    hid, chan = weight.shape[1], weight.shape[2]
    cols = out_cols
    w = weight.reshape(3, 3, hid, chan).transpose(0, 1, 3, 2)
    if first:
        w = w.reshape(3, 3 * chan, hid)
        w = jnp.pad(w, ((0, 0), (0, cols - 3 * chan), (0, 0)))
    else:
        w = w.reshape(3, 3 * chan, hid)
    width = w.shape[1]
    zero = jnp.zeros((width, hid), w.dtype)
    wide = [
        jnp.concatenate([w[a] if a < 3 else zero, w[a - 1] if a > 0 else zero], axis=1)
        for a in range(4)
    ]
    wa = jnp.concatenate(wide[:2], axis=0)
    wb = jnp.concatenate(wide[2:], axis=0)
    scratch = [
        pltpu.VMEM((rows // 2 + 1, cols, 2 * width), BF),
        pltpu.VMEM((2, cols + 16, cols), F32),
    ]
    if first:
        bias_in = jnp.concatenate([bias, bias])[None, :]
        bias_spec = pl.BlockSpec((1, 2 * hid), lambda f: (0, 0))
        out_shape = jax.ShapeDtypeStruct((face_count * rows, cols, hid), BF)
        out_spec = pl.BlockSpec((rows, cols, hid), lambda f: (f, 0, 0))
    else:
        bias_in = bias
        bias_spec = pl.BlockSpec(memory_space=pltpu.SMEM)
        out_shape = jax.ShapeDtypeStruct((hid, face_count, rows, cols), BF)
        out_spec = pl.BlockSpec((hid, 1, rows, cols), lambda f: (0, f, 0, 0))
        scratch.append(pltpu.VMEM((hid * 2 * PAIRS, cols), F32))
    return pl.pallas_call(
        functools.partial(conv_kernel, first),
        out_shape=out_shape,
        grid=(face_count,),
        in_specs=[
            pl.BlockSpec((rows,) + x.shape[1:], lambda f: (f, 0, 0)),
            pl.BlockSpec((1,) + top.shape[1:], lambda f: (f, 0, 0)),
            pl.BlockSpec((1,) + bot.shape[1:], lambda f: (f, 0, 0)),
            pl.BlockSpec((1,) + left.shape[1:], lambda f: (f, 0, 0)),
            pl.BlockSpec((1,) + right.shape[1:], lambda f: (f, 0, 0)),
            pl.BlockSpec(wa.shape, lambda f: (0, 0)),
            pl.BlockSpec(wb.shape, lambda f: (0, 0)),
            bias_spec,
        ],
        out_specs=out_spec,
        scratch_shapes=scratch,
        compiler_params=pltpu.CompilerParams(vmem_limit_bytes=VMEM_LIMIT),
        name="conv1" if first else "conv2",
    )(x, top, bot, left, right, wa, wb, bias_in)


def halos_of(top, bottom, left, right, seam_table):
    faces, cols, chan = top.shape
    rows = left.shape[1]
    nb, nt = lax.axis_size("band"), lax.axis_size("tile")
    band, tile = lax.axis_index("band"), lax.axis_index("tile")
    side = cols * nt

    row_edge = jnp.where(band == 0, top, bottom).reshape(nb, faces * cols // nb, chan)
    col_edge = jnp.where(tile == 0, left, right).reshape(nt, faces * rows // nt, chan)
    row_part = lax.all_to_all(row_edge, "band", 0, 0, tiled=True)
    col_part = lax.all_to_all(col_edge, "tile", 0, 0, tiled=True)
    mine = jnp.concatenate([row_part[0], row_part[-1], col_part[0], col_part[-1]], axis=0)
    rp, cp = row_edge.shape[1], col_edge.shape[1]
    every = lax.all_gather(mine, ("band", "tile"), axis=0, tiled=False)
    every = every.reshape(nb, nt, 2 * rp + 2 * cp, chan)
    row_all = every[:, :, : 2 * rp].reshape(nb, nt, 2, rp, chan)
    row_all = row_all.transpose(2, 0, 3, 1, 4).reshape(2, faces, cols, nt, chan)
    row_all = row_all.transpose(1, 0, 3, 2, 4).reshape(faces, 2, side, chan)
    col_all = every[:, :, 2 * rp :].reshape(nb, nt, 2, cp, chan)
    col_all = col_all.transpose(2, 1, 3, 0, 4).reshape(2, faces, rows, nb, chan)
    col_all = col_all.transpose(1, 0, 3, 2, 4).reshape(faces, 2, side, chan)
    lines = jnp.concatenate([row_all, col_all], axis=1).reshape(faces * 4, side, chan)
    lines = jnp.pad(lines, ((0, 0), (1, 1), (0, 0)))

    def segments(which, start, length):
        index = seam_table[:, which, 0] * 4 + seam_table[:, which, 1]
        rev = seam_table[:, which, 2] == 1
        first = jnp.where(rev, side - start - length, start)
        got = jax.vmap(
            lambda i, s: lax.dynamic_slice(lines, (i, s, 0), (1, length + 2, chan))[0]
        )(index, first)
        flip = jnp.eye(length + 2, dtype=BF)[::-1]
        flipped = jnp.einsum("pq,fqc->fpc", flip, got, preferred_element_type=F32).astype(BF)
        return jnp.where(rev[:, None, None], flipped, got)

    def shift(x, axis, size, forward):
        pairs = [(i, i + 1) if forward else (i + 1, i) for i in range(size - 1)]
        return lax.ppermute(x, axis, pairs)

    above = shift(bottom, "band", nb, True)
    below = shift(top, "band", nb, False)
    ext_left = jnp.concatenate([above[:, :1], left, below[:, :1]], axis=1)
    ext_right = jnp.concatenate([above[:, -1:], right, below[:, -1:]], axis=1)
    from_left = shift(ext_right, "tile", nt, True)
    from_right = shift(ext_left, "tile", nt, False)
    lefts = jnp.where(tile == 0, segments(2, band * rows, rows), from_left)
    rights = jnp.where(tile == nt - 1, segments(3, band * rows, rows), from_right)

    def line(at_edge, seam, inner, at):
        seam = jnp.concatenate([seam[:, 1:-1], seam[:, :1], seam[:, -1:]], axis=1)
        inner = jnp.concatenate([inner, lefts[:, at : at + 1], rights[:, at : at + 1]], axis=1)
        return jnp.where(at_edge, seam, inner)

    tops = line(band == 0, segments(0, tile * cols, cols), above, 0)
    bots = line(band == nb - 1, segments(1, tile * cols, cols), below, rows + 1)
    return tops, bots, lefts[:, 1:-1].astype(F32), rights[:, 1:-1].astype(F32)


def local(
    source,
    regrid_weights,
    dest_group,
    dest_block,
    seam_table,
    conv1_weight,
    conv1_bias,
    conv2_weight,
    conv2_bias,
):
    fields = source.shape[0]
    src_count, top_count, block_len, _ = regrid_weights.shape
    nb, nt = lax.axis_size("band"), lax.axis_size("tile")
    devices = nb * nt
    capacity = 3 * src_count * top_count // devices
    rows = block_len * nt // nb
    faces = seam_table.shape[0]
    slots_dev = faces * rows
    items = src_count * top_count
    target_dev = dest_group.reshape(items)
    target_slot = dest_block.reshape(items)
    onehot = (target_dev[:, None] == jnp.arange(devices, dtype=jnp.int32)[None, :]).astype(F32)
    earlier = (jnp.arange(items)[:, None] > jnp.arange(items)[None, :]).astype(BF)
    before = jnp.dot(earlier, onehot.astype(BF), preferred_element_type=F32)
    rank_in = jnp.sum(before * onehot, axis=1).astype(jnp.int32)
    position = target_dev * capacity + rank_in
    hit = position[None, :] == jnp.arange(devices * capacity, dtype=jnp.int32)[:, None]
    out_slots = slots_dev + jnp.sum(jnp.where(hit, target_slot[None, :] - slots_dev, 0), axis=1)
    outgoing = partials(position, source, regrid_weights, devices * capacity)
    axes = ("band", "tile")
    arrived = lax.all_to_all(
        outgoing.reshape(devices, capacity, fields, block_len), axes, 0, 0, tiled=True
    )
    arrived_slots = lax.all_to_all(
        out_slots.reshape(devices, capacity), axes, 0, 0, tiled=True
    )
    grid = collect(
        arrived_slots.reshape(-1), arrived.reshape(devices * capacity, fields, block_len), slots_dev
    )
    tiles = grid.reshape(faces, rows, fields, block_len)
    halos = halos_of(
        tiles[:, 0].transpose(0, 2, 1),
        tiles[:, -1].transpose(0, 2, 1),
        tiles[:, :, :, 0],
        tiles[:, :, :, -1],
        seam_table,
    )
    hidden = conv(True, grid, halos, conv1_weight, conv1_bias, faces, rows, block_len)
    tiles = hidden.reshape(faces, rows, block_len, hidden.shape[2])
    halos = halos_of(
        tiles[:, 0], tiles[:, -1], tiles[:, :, 0], tiles[:, :, -1], seam_table
    )
    return conv(False, hidden, halos, conv2_weight, conv2_bias, faces, rows, block_len)


def solution(mesh):
    return jax.shard_map(
        local,
        mesh=mesh,
        in_specs=(
            P(None, ("band", "tile")),
            P(("band", "tile"), None, None, None),
            P(("band", "tile"), None),
            P(("band", "tile"), None),
            P(),
            P(),
            P(),
            P(),
            P(),
        ),
        out_specs=P(None, None, "band", "tile"),
        check_vma=False,
    )
```

```python
import functools

import jax
import jax.numpy as jnp
from jax import lax
from jax.experimental import pallas as pl
from jax.experimental.pallas import tpu as pltpu
from jax.sharding import PartitionSpec as P

BF = jnp.bfloat16
F32 = jnp.float32
VMEM_LIMIT = 60 * 1024 * 1024
PAIRS = 8
UNROLLED = True
GELU_COEF = (
    0.7978842684146765,
    0.03633414911622174,
    -3.30267008968913e-05,
    -5.527338755532785e-05,
    3.974071022505988e-06,
    -1.3378322650770525e-07,
    1.8139281733930472e-09,
)
GELU_CAP = 30.0


def gelu(v):
    u = jnp.minimum(v * v, GELU_CAP)
    q = jnp.full_like(u, GELU_COEF[-1])
    for c in GELU_COEF[-2::-1]:
        q = q * u + c
    half = 0.5 * v
    return half + half * jnp.tanh(v * q)


def partial_kernel(pos_ref, src_ref, w_ref, out_ref):
    s = pl.program_id(0)
    per_step = w_ref.shape[0]
    top, blk = w_ref.shape[1], w_ref.shape[2]

    @pl.when(s == 0)
    def _():
        out_ref[...] = jnp.zeros_like(out_ref)

    for j in range(per_step):
        x = src_ref[:, j * blk : (j + 1) * blk]
        for k in range(top):
            y = jnp.dot(x, w_ref[j, k], preferred_element_type=F32).astype(BF)
            out_ref[pos_ref[(s * per_step + j) * top + k]] = y


def partials(position, source, weights, slots):
    fields = source.shape[0]
    src_count, top, blk, _ = weights.shape
    step = 4
    return pl.pallas_call(
        partial_kernel,
        out_shape=jax.ShapeDtypeStruct((slots, fields, blk), BF),
        grid_spec=pltpu.PrefetchScalarGridSpec(
            num_scalar_prefetch=1,
            grid=(src_count // step,),
            in_specs=[
                pl.BlockSpec((fields, step * blk), lambda i, p: (0, i)),
                pl.BlockSpec((step, top, blk, blk), lambda i, p: (i, 0, 0, 0)),
            ],
            out_specs=pl.BlockSpec((slots, fields, blk), lambda i, p: (0, 0, 0)),
        ),
        compiler_params=pltpu.CompilerParams(vmem_limit_bytes=VMEM_LIMIT),
        name="partials",
    )(position, source, weights)


def collect_kernel(slot_ref, arr_ref, out_ref, acc_ref):
    i = pl.program_id(0)
    n = arr_ref.shape[0]

    @pl.when(i == 0)
    def _():
        acc_ref[...] = jnp.zeros_like(acc_ref)

    def body(j, _):
        slot = slot_ref[i * n + j]
        acc_ref[slot] = acc_ref[slot] + arr_ref[j].astype(F32)
        return 0

    lax.fori_loop(0, n, body, 0, unroll=4)

    @pl.when(i == pl.num_programs(0) - 1)
    def _():
        out_ref[...] = acc_ref[: out_ref.shape[0]].astype(BF)


def collect(slots, arrived, slots_dev):
    count, fields, blk = arrived.shape
    steps = 8
    return pl.pallas_call(
        collect_kernel,
        out_shape=jax.ShapeDtypeStruct((slots_dev, fields, blk), BF),
        grid_spec=pltpu.PrefetchScalarGridSpec(
            num_scalar_prefetch=1,
            grid=(steps,),
            in_specs=[pl.BlockSpec((count // steps, fields, blk), lambda i, p: (i, 0, 0))],
            out_specs=pl.BlockSpec((slots_dev, fields, blk), lambda i, p: (0, 0, 0)),
            scratch_shapes=[pltpu.VMEM((slots_dev + 1, fields, blk), F32)],
        ),
        compiler_params=pltpu.CompilerParams(vmem_limit_bytes=VMEM_LIMIT),
        name="collect",
    )(slots, arrived)


def conv_kernel(
    first, x_ref, top_ref, bot_ref, left_ref, right_ref, wa_ref, wb_ref, b_ref, out_ref, *scratch
):
    if first:
        ends, scratch = scratch[0], scratch[1:]
    sl, win = scratch[0], scratch[1]
    rows = out_ref.shape[0] if first else out_ref.shape[2]
    cols = sl.shape[1]
    width = sl.shape[2] // 2
    chan = left_ref.shape[-1]
    slots = win.shape[0]

    def put(slot, pair, parity, row32, lo, hi):
        win[slot, 8 : 8 + cols, :] = row32
        win[slot, 7:8, :] = lo
        win[slot, 8 + cols : 9 + cols, :] = hi
        before = win[slot, 7 : 7 + cols, :]
        after = win[slot, 9 : 9 + cols, :]
        base = parity * width
        if first:
            g = before + pltpu.roll(row32, chan, 1) + pltpu.roll(after, 2 * chan, 1)
            sl[pair, :, base : base + width] = g.astype(BF)
        else:
            sl[pair, :, base : base + cols] = before.astype(BF)
            sl[pair, :, base + cols : base + 2 * cols] = row32.astype(BF)
            sl[pair, :, base + 2 * cols : base + 3 * cols] = after.astype(BF)

    def wide(v):
        if first:
            v = jnp.concatenate([v, jnp.zeros((v.shape[0], cols - chan), v.dtype)], axis=1)
        return v

    def row_at(r):
        if first:
            y = x_ref[r].astype(F32)
            y = jnp.concatenate([y, jnp.zeros((cols - chan, cols), F32)], axis=0)
            return y.T
        return x_ref[r].astype(F32)

    def halo_row(ref):
        full = wide(ref[0].astype(F32))
        return full[:cols], full[cols : cols + 1], full[cols + 1 : cols + 2]

    def put_row(r, k):
        put(
            k % slots,
            r // 2 + k % 2 if isinstance(r, int) else (r - k % 2) // 2 + k % 2,
            1 - k % 2,
            row_at(r),
            wide(left_ref[0, pl.ds(r, 1), :]),
            wide(right_ref[0, pl.ds(r, 1), :]),
        )

    row, lo, hi = halo_row(top_ref)
    put(0, 0, 0, row, lo, hi)
    row, lo, hi = halo_row(bot_ref)
    put(1, rows // 2, 1, row, lo, hi)
    unroll = UNROLLED
    n = 2 * PAIRS

    def fill_loop(i, _):
        for k in range(slots):
            put_row(i * slots + k, k)
        return 0

    def dots(p0):
        a = sl[pl.ds(p0, PAIRS)].reshape(PAIRS * cols, 2 * width)
        b = sl[pl.ds(p0 + 1, PAIRS)].reshape(PAIRS * cols, 2 * width)
        return jnp.dot(a, wa_ref[...], preferred_element_type=F32) + jnp.dot(
            b, wb_ref[...], preferred_element_type=F32
        )

    def finish(g, y):
        p0 = g * PAIRS
        hid = y.shape[1] // 2
        if first:
            y = gelu(y + b_ref[...])
            for p in range(PAIRS):
                for q in range(2):
                    part = y[p * cols : (p + 1) * cols, q * hid : (q + 1) * hid].astype(BF)
                    r = 2 * (p0 + p) + q
                    out_ref[r] = part
                    ends[0, 0, pl.ds(r, 1), :] = part[:1].astype(F32)
                    ends[1, 0, pl.ds(r, 1), :] = part[cols - 1 :].astype(F32)
            return
        flip = scratch[2].at[g % 2 if unroll else 0]
        for p in range(PAIRS):
            for q in range(2):
                part = y[p * cols : (p + 1) * cols, q * hid : (q + 1) * hid]
                flip[pl.ds(2 * p + q, hid, stride=n), :] = part.T

        def group(o, _):
            for j in range(8):
                v = flip[pl.ds((o * 8 + j) * n, n), :]
                out_ref[o * 8 + j, 0, pl.ds(g * n, n), :] = gelu(v + b_ref[o * 8 + j]).astype(BF)
            return 0

        if unroll:
            for o in range(hid // 8):
                group(o, 0)
        else:
            lax.fori_loop(0, hid // 8, group, 0)

    if unroll:
        for k in range(min(n + 2, rows)):
            put_row(k, k)
        for g in range(rows // n):
            y = dots(g * PAIRS)
            for k in range((g + 1) * n + 2, min((g + 2) * n + 2, rows)):
                put_row(k, k)
            finish(g, y)
    else:
        lax.fori_loop(0, rows // slots, fill_loop, 0)

        def chunk(g, _):
            finish(g, dots(g * PAIRS))
            return 0

        lax.fori_loop(0, rows // n, chunk, 0)


def conv(first, x, halos, weight, bias, face_count, rows, out_cols):
    top, bot, left, right = halos
    hid, chan = weight.shape[1], weight.shape[2]
    cols = out_cols
    w = weight.reshape(3, 3, hid, chan).transpose(0, 1, 3, 2)
    if first:
        w = w.reshape(3, 3 * chan, hid)
        w = jnp.pad(w, ((0, 0), (0, cols - 3 * chan), (0, 0)))
    else:
        w = w.reshape(3, 3 * chan, hid)
    width = w.shape[1]
    zero = jnp.zeros((width, hid), w.dtype)
    wide = [
        jnp.concatenate([w[a] if a < 3 else zero, w[a - 1] if a > 0 else zero], axis=1)
        for a in range(4)
    ]
    wa = jnp.concatenate(wide[:2], axis=0)
    wb = jnp.concatenate(wide[2:], axis=0)
    scratch = [
        pltpu.VMEM((rows // 2 + 1, cols, 2 * width), BF),
        pltpu.VMEM((8, cols + 16, cols), F32),
    ]
    if first:
        bias_in = jnp.concatenate([bias, bias])[None, :]
        bias_spec = pl.BlockSpec((1, 2 * hid), lambda f: (0, 0))
        out_shape = (
            jax.ShapeDtypeStruct((face_count * rows, cols, hid), BF),
            jax.ShapeDtypeStruct((2, face_count, rows, hid), F32),
        )
        out_spec = (
            pl.BlockSpec((rows, cols, hid), lambda f: (f, 0, 0)),
            pl.BlockSpec((2, 1, rows, hid), lambda f: (0, f, 0, 0)),
        )
    else:
        bias_in = bias
        bias_spec = pl.BlockSpec(memory_space=pltpu.SMEM)
        out_shape = jax.ShapeDtypeStruct((hid, face_count, rows, cols), BF)
        out_spec = pl.BlockSpec((hid, 1, rows, cols), lambda f: (0, f, 0, 0))
        scratch.append(pltpu.VMEM((2, hid * 2 * PAIRS, cols), F32))
    return pl.pallas_call(
        functools.partial(conv_kernel, first),
        out_shape=out_shape,
        grid=(face_count,),
        in_specs=[
            pl.BlockSpec((rows,) + x.shape[1:], lambda f: (f, 0, 0)),
            pl.BlockSpec((1,) + top.shape[1:], lambda f: (f, 0, 0)),
            pl.BlockSpec((1,) + bot.shape[1:], lambda f: (f, 0, 0)),
            pl.BlockSpec((1,) + left.shape[1:], lambda f: (f, 0, 0)),
            pl.BlockSpec((1,) + right.shape[1:], lambda f: (f, 0, 0)),
            pl.BlockSpec(wa.shape, lambda f: (0, 0)),
            pl.BlockSpec(wb.shape, lambda f: (0, 0)),
            bias_spec,
        ],
        out_specs=out_spec,
        scratch_shapes=scratch,
        compiler_params=pltpu.CompilerParams(vmem_limit_bytes=VMEM_LIMIT),
        name="conv1" if first else "conv2",
    )(x, top, bot, left, right, wa, wb, bias_in)


def halos_of(top, bottom, left, right, seam_table):
    faces, cols, chan = top.shape
    rows = left.shape[1]
    nb, nt = lax.axis_size("band"), lax.axis_size("tile")
    band, tile = lax.axis_index("band"), lax.axis_index("tile")
    side = cols * nt

    row_edge = jnp.where(band == 0, top, bottom).reshape(nb, faces * cols // nb, chan)
    col_edge = jnp.where(tile == 0, left, right).reshape(nt, faces * rows // nt, chan)
    row_part = lax.all_to_all(row_edge, "band", 0, 0, tiled=True)
    col_part = lax.all_to_all(col_edge, "tile", 0, 0, tiled=True)
    mine = jnp.concatenate([row_part[0], row_part[-1], col_part[0], col_part[-1]], axis=0)
    every = lax.all_gather(mine, ("band", "tile"), axis=0, tiled=False)
    pieces = every.reshape(-1, rows, chan)
    per_row, per_col = row_edge.shape[1] // rows, col_edge.shape[1] // rows
    per_dev = 2 * (per_row + per_col)
    per_tile = cols // rows
    last_piece = side // rows - 1

    def wanted(which, first, count):
        at = first - 1 + jnp.arange(count + 2, dtype=jnp.int32)
        face = seam_table[:, which, 0][:, None]
        edge = seam_table[:, which, 1][:, None]
        rev = seam_table[:, which, 2][:, None] == 1
        q = jnp.clip(jnp.where(rev, last_piece - at, at), 0, last_piece)
        c = face * per_tile + q % per_tile
        on_row = (c // per_row * nt + q // per_tile) * per_dev + edge * per_row + c % per_row
        on_col = (
            (q * nt + face // per_col) * per_dev
            + 2 * per_row
            + (edge - 2) * per_col
            + face % per_col
        )
        return jnp.where(edge < 2, on_row, on_col), jnp.broadcast_to(rev, q.shape)

    asked = [
        (0, tile * per_tile, per_tile),
        (1, tile * per_tile, per_tile),
        (2, band, 1),
        (3, band, 1),
    ]
    parts = [wanted(*a) for a in asked]
    index = jnp.concatenate([p[0] for p in parts], axis=1)
    rev = jnp.concatenate([p[1] for p in parts], axis=1)
    got = jnp.take(pieces, index.reshape(-1), axis=0, mode="clip")
    flip = jnp.eye(rows, dtype=BF)[::-1]
    flipped = jnp.einsum("pq,kqc->kpc", flip, got, preferred_element_type=F32).astype(BF)
    got = jnp.where(rev.reshape(-1)[:, None, None], flipped, got)
    got = got.reshape(faces, index.shape[1], rows, chan)
    offset = [0]
    for a in asked:
        offset.append(offset[-1] + a[2] + 2)

    def segments(which):
        o, n, first = offset[which], asked[which][2], asked[which][1]
        middle = got[:, o + 1 : o + 1 + n].reshape(faces, n * rows, chan)
        lead = jnp.where(first > 0, got[:, o, -1:], 0)
        trail = jnp.where(first + n <= last_piece, got[:, o + 1 + n, :1], 0)
        return lead, middle, trail

    def shift(x, axis, size, forward):
        pairs = [(i, i + 1) if forward else (i + 1, i) for i in range(size - 1)]
        return lax.ppermute(x, axis, pairs)

    above = shift(bottom, "band", nb, True)
    below = shift(top, "band", nb, False)
    ext_left = jnp.concatenate([above[:, :1], left, below[:, :1]], axis=1)
    ext_right = jnp.concatenate([above[:, -1:], right, below[:, -1:]], axis=1)
    from_left = shift(ext_right, "tile", nt, True)
    from_right = shift(ext_left, "tile", nt, False)
    lefts = jnp.where(tile == 0, jnp.concatenate(segments(2), axis=1), from_left)
    rights = jnp.where(tile == nt - 1, jnp.concatenate(segments(3), axis=1), from_right)

    def line(at_edge, which, inner, at):
        lead, middle, trail = segments(which)
        lead = jnp.where(at_edge, lead, lefts[:, at : at + 1])
        trail = jnp.where(at_edge, trail, rights[:, at : at + 1])
        return jnp.concatenate([jnp.where(at_edge, middle, inner), lead, trail], axis=1)

    tops = line(band == 0, 0, above, 0)
    bots = line(band == nb - 1, 1, below, rows + 1)
    return tops, bots, lefts[:, 1:-1].astype(F32), rights[:, 1:-1].astype(F32)


def local(
    source,
    regrid_weights,
    dest_group,
    dest_block,
    seam_table,
    conv1_weight,
    conv1_bias,
    conv2_weight,
    conv2_bias,
):
    fields = source.shape[0]
    src_count, top_count, block_len, _ = regrid_weights.shape
    nb, nt = lax.axis_size("band"), lax.axis_size("tile")
    devices = nb * nt
    capacity = 3 * src_count * top_count // devices
    rows = block_len * nt // nb
    faces = seam_table.shape[0]
    slots_dev = faces * rows
    items = src_count * top_count
    target_dev = dest_group.reshape(items)
    target_slot = dest_block.reshape(items)
    onehot = (target_dev[:, None] == jnp.arange(devices, dtype=jnp.int32)[None, :]).astype(F32)
    earlier = (jnp.arange(items)[:, None] > jnp.arange(items)[None, :]).astype(BF)
    before = jnp.dot(earlier, onehot.astype(BF), preferred_element_type=F32)
    rank_in = jnp.sum(before * onehot, axis=1).astype(jnp.int32)
    position = target_dev * capacity + rank_in
    hit = position[None, :] == jnp.arange(devices * capacity, dtype=jnp.int32)[:, None]
    out_slots = slots_dev + jnp.sum(jnp.where(hit, target_slot[None, :] - slots_dev, 0), axis=1)
    outgoing = partials(position, source, regrid_weights, devices * capacity)
    axes = ("band", "tile")
    arrived = lax.all_to_all(
        outgoing.reshape(devices, capacity, fields, block_len), axes, 0, 0, tiled=True
    )
    arrived_slots = lax.all_to_all(
        out_slots.reshape(devices, capacity), axes, 0, 0, tiled=True
    )
    grid = collect(
        arrived_slots.reshape(-1), arrived.reshape(devices * capacity, fields, block_len), slots_dev
    )
    tiles = grid.reshape(faces, rows, fields, block_len)
    pick = jnp.eye(block_len, dtype=BF)[jnp.array([0, block_len - 1])]
    ends = jnp.einsum("ep,tcp->etc", pick, grid, preferred_element_type=F32).astype(BF)
    ends = ends.reshape(2, faces, rows, fields)
    halos = halos_of(
        tiles[:, 0].transpose(0, 2, 1),
        tiles[:, -1].transpose(0, 2, 1),
        ends[0],
        ends[1],
        seam_table,
    )
    hidden, ends = conv(True, grid, halos, conv1_weight, conv1_bias, faces, rows, block_len)
    tiles = hidden.reshape(faces, rows, block_len, hidden.shape[2])
    halos = halos_of(
        tiles[:, 0], tiles[:, -1], ends[0].astype(BF), ends[1].astype(BF), seam_table
    )
    return conv(False, hidden, halos, conv2_weight, conv2_bias, faces, rows, block_len)


def solution(mesh):
    return jax.shard_map(
        local,
        mesh=mesh,
        in_specs=(
            P(None, ("band", "tile")),
            P(("band", "tile"), None, None, None),
            P(("band", "tile"), None),
            P(("band", "tile"), None),
            P(),
            P(),
            P(),
            P(),
            P(),
        ),
        out_specs=P(None, None, "band", "tile"),
        check_vma=False,
    )
```
